512 devices in a mesh: grp: 16 (over z, core), dev: 32 (over y, x).
Axes of the slice: x: 4, y: 8, z: 8, core: 2. Of those that a mesh axis runs over, the one named last changes fastest.
Arguments:
- stored_tiles: float32 [512, 33, 128, 128], P(('grp', 'dev')), may hold values from -0.22097087 to 0.22097087, as said below
- tile_flags: int32 [512, 33], P(('grp', 'dev')), may hold values from 0 to 1, as said below
- orbitals: float32 [65536, 256], P(('grp', 'dev')), may hold values from -6 to 6
Outputs:
- product: float32 [65536, 256], P(('grp', 'dev'))
The draws below stay inside these ranges and needn't reach their ends.
Inputs may be any that keep to these rules, and one draw needn't show every extreme that they name: tile_flags[p, s] is 1 at s = p mod 32, 0 for s below that, and 0 at s = 32 in the last 32 block rows. `stored_tiles`: the tile at slot p mod 32 of block row p is symmetric.
All inputs are finite; a program needn't handle non-finite values.
Results may differ from the reference program's by a relative error of at most 0.000075.
Values sent between devices are 32-bit elements; how exact they have to be, the bound alone decides.
A program may use at most 64 MiB of HBM per device.

```python
import math
import jax
import jax.numpy as jnp
from jax import lax

B = 128
K = 256
SLOTS = 33
NB = 512
ROWS = 65536


def draw_stored_tiles(key, part):
    spread = 0.25 / math.sqrt(B)
    full_shape = (NB, SLOTS, B, B)
    entries = jax.random.truncated_normal(key, -4.0, 4.0, full_shape, jnp.float32)
    row_index = lax.broadcasted_iota(jnp.int32, (NB, SLOTS, 1, 1), 0) % (SLOTS - 1)
    slot_index = lax.broadcasted_iota(jnp.int32, (NB, SLOTS, 1, 1), 1)
    mirrored = (entries + jnp.swapaxes(entries, 2, 3)) * 0.70710678
    return jnp.where(row_index == slot_index, mirrored, entries) * spread


def draw_tile_flags(key, part):
    group_width = SLOTS - 1
    coin_flips = jax.random.randint(key, (NB, SLOTS), 0, 2)
    row_index = lax.broadcasted_iota(jnp.int32, (NB, SLOTS), 0)
    slot_index = lax.broadcasted_iota(jnp.int32, (NB, SLOTS), 1)
    own_slot = row_index % group_width
    result = jnp.where(slot_index == own_slot, 1, jnp.where(slot_index < own_slot, 0, coin_flips))
    last_group = row_index >= NB - group_width
    result = jnp.where((slot_index == group_width) & last_group, 0, result)
    return result.astype(jnp.int32)


def steps_of(stream_key, dims, cuts, low, top_value):
    factor_of, own = 1.0, jax.random.fold_in(stream_key, 6)
    for axis_at, parts in cuts:
        heights = jnp.exp(jax.random.uniform(jax.random.fold_in(own, axis_at), (parts,), jnp.float32, low / len(cuts), top_value / len(cuts)))
        factor_of = factor_of * jnp.repeat(heights, dims[axis_at] // parts).reshape([-1 if axis == axis_at else 1 for axis in range(len(dims))])
    return factor_of


def scatter_about(own_key, shape, deviation, reach, cuts=(), kind=jnp.bfloat16):
    drawn = deviation * jax.random.normal(own_key, shape, jnp.float32)
    if cuts:
        drawn = drawn * steps_of(own_key, shape, cuts, -0.22, 0.18)
    return jnp.clip(drawn, -reach, reach).astype(kind)


def setup_inputs(seed: int = 0) -> dict:
    seeds = jax.random.split(jax.random.key(seed), 4)
    stored_tiles = draw_stored_tiles(jax.random.fold_in(seeds[3], 71), 0)
    tile_flags = draw_tile_flags(jax.random.fold_in(seeds[3], 71), 0)
    orbitals = scatter_about(seeds[2], (ROWS, K), 1.0, 6.0, ((0, 512),), jnp.float32)
    return {"stored_tiles": stored_tiles, "tile_flags": tile_flags, "orbitals": orbitals}


def reference(stored_tiles, tile_flags, orbitals):
    group_width = SLOTS - 1
    groups = NB // group_width
    highest = lax.Precision.HIGHEST
    tile_groups = stored_tiles.reshape(groups, group_width, SLOTS, B, B)
    flag_groups = tile_flags.reshape(groups, group_width, SLOTS)
    orbital_groups = orbitals.reshape(groups, group_width, B, K)
    following = jnp.concatenate([orbital_groups[1:], jnp.zeros((1, group_width, B, K), orbitals.dtype)], 0)
    offdiag = 1.0 - jnp.eye(group_width, dtype=orbitals.dtype)

    def one_group(inputs):
        group_tiles, group_flags, x_here, x_after = inputs
        blocks = group_tiles * group_flags.astype(group_tiles.dtype)[:, :, None, None]
        in_group = blocks[:, :group_width]
        next_tile = blocks[:, group_width]
        direct = jnp.einsum("dsij,sjk->dik", in_group, x_here, precision=highest)
        beside = in_group * offdiag[:, :, None, None]
        mirror = jnp.einsum("dsij,dik->sjk", beside, x_here, precision=highest)
        forward = jnp.einsum("dij,djk->dik", next_tile, x_after, precision=highest)
        upward = jnp.einsum("dij,dik->djk", next_tile, x_here, precision=highest)
        return direct + mirror + forward, upward

    in_sums, upward = lax.map(one_group, (tile_groups, flag_groups, orbital_groups, following))
    shifted = jnp.concatenate([jnp.zeros((1, group_width, B, K), orbitals.dtype), upward[:-1]], 0)
    return (in_sums + shifted).reshape(NB * B, K)
```

```python
import jax
import jax.numpy as jnp
from jax import lax
from jax.experimental import pallas as pl
from jax.experimental.pallas import tpu as pltpu
from jax.sharding import PartitionSpec as P

MESH = pl.DeviceIdType.MESH
NX = 4
NY = 8


def split(v):
    high = v.astype(jnp.bfloat16)
    return high, (v - high.astype(jnp.float32)).astype(jnp.bfloat16)


def multiply(a, b, dims):
    def one(u, v):
        return lax.dot_general(u, v, (dims, ((), ())), preferred_element_type=jnp.float32)

    return one(a[0], b[0]) + (one(a[0], b[1]) + one(a[1], b[0]))


PLAIN = ((1,), (0,))
TURNED = ((0,), (0,))


def kernel(
    tiles, flags, orb, out,
    own, held, xrow, xrow_high, xrow_low, xcol, total, mirror_out, mirror_in, direct_in, x_next, up_out, up_in,
    load_sem, tile_send, tile_recv, xrow_send, xrow_recv, xcol_send, xcol_recv,
    mirror_send, mirror_recv, direct_send, direct_recv, next_send, next_recv,
):
    order = tiles.shape[1]
    slots = tiles.shape[0]
    groups = lax.axis_size("grp")
    g, d = lax.axis_index("grp"), lax.axis_index("dev")
    y, x = d // NX, d % NX

    def in_row(j):
        return {"dev": y * NX + (x + j) % NX}

    def in_column(k):
        return {"dev": (y + k) * NX + x}

    def block(i):
        return pl.ds(pl.multiple_of(i * order, order), order)

    def remote(src, dst, send, recv, device):
        return pltpu.make_async_remote_copy(
            src_ref=src, dst_ref=dst, send_sem=send, recv_sem=recv, device_id=device, device_id_type=MESH
        )

    def tile_copy(j, k):
        return remote(
            own.at[(y + k) * NX + (x + j) % NX], held.at[k, block(x)],
            tile_send.at[j, k], tile_recv.at[j, k], in_row(j),
        )

    def xrow_copy(j):
        return remote(orb, xrow.at[block(x)], xrow_send.at[j], xrow_recv.at[j], in_row(j))

    def xcol_copy(k):
        return remote(orb, xcol.at[k], xcol_send.at[k], xcol_recv.at[k], in_column(-k))

    def mirror_copy(k):
        return remote(mirror_out.at[k], mirror_in.at[k], mirror_send.at[k], mirror_recv.at[k], in_column(k))

    def direct_copy(j):
        return remote(
            total.at[block((x + j) % NX)], direct_in.at[j], direct_send.at[j], direct_recv.at[j], in_row(j)
        )

    def back_copy():
        return remote(orb, x_next, next_send.at[0], next_recv.at[0], {"grp": g - 1})

    def up_copy():
        return remote(up_out, up_in, next_send.at[1], next_recv.at[1], {"grp": g + 1})

    def step_of(i):
        return (4 + jnp.where(i % 2 == 1, (i + 1) // 2, -(i // 2)) + NY) % NY

    load_tiles = pltpu.make_async_copy(tiles, own, load_sem.at[0])
    load_row = pltpu.make_async_copy(orb, xrow.at[block(x)], load_sem.at[1])
    load_col = pltpu.make_async_copy(orb, xcol.at[0], load_sem.at[2])
    load_tiles.start()
    load_row.start()
    load_col.start()
    held[0] = jnp.zeros_like(held[0])

    barrier = pltpu.get_barrier_semaphore()
    for j in range(1, NX):
        pl.semaphore_signal(barrier, inc=1, device_id=in_row(j), device_id_type=MESH)
    for k in range(1, NY):
        pl.semaphore_signal(
            barrier, inc=1, device_id={"dev": ((y + k) % NY) * NX + x}, device_id_type=MESH
        )

    for i in (1, groups - 1):
        pl.semaphore_signal(
            barrier, inc=1, device_id={"grp": (g + i) % groups}, device_id_type=MESH
        )

    load_tiles.wait()

    def mask(s, carry):
        own[s] = own[s] * flags[0, s].astype(jnp.float32)
        return carry

    lax.fori_loop(y * NX, slots, mask, 0)

    pl.semaphore_wait(barrier, NX - 1 + NY - 1 + 2)

    for j in range(1, NX):
        xrow_copy(j).start()

    def send_xcol(i, carry):
        k = step_of(i)

        @pl.when(k <= y)
        def _():
            xcol_copy(k).start()

        return carry

    lax.fori_loop(0, NY - 1, send_xcol, 0)

    @pl.when(g > 0)
    def _():
        back_copy().start()

    def send_tiles(i, carry):
        k = step_of(i)

        @pl.when(y + k < NY)
        def _():
            for j in range(1, NX):
                tile_copy(j, k).start()

        return carry

    lax.fori_loop(0, NY - 1, send_tiles, 0)
    for j in range(1, NX):

        @pl.when(x + j < NX)
        def _():
            tile_copy(j, 0).start()

    load_row.wait()
    load_col.wait()
    x_own = split(xcol[0])

    @pl.when(g < groups - 1)
    def _():
        up_out[...] = multiply(split(own[slots - 1]), x_own, TURNED)
        up_copy().start()

    def place(k, carry):
        held[k, block(x)] = own[(y + k) * NX + x]
        return carry

    lax.fori_loop(0, NY - y, place, 0)
    total[...] = jnp.zeros_like(total)
    for j in range(1, NX):
        xrow_copy(j).wait_recv()
    xrow_high[...], xrow_low[...] = split(xrow[...])

    def step(i, carry):
        k = step_of(i)

        @pl.when(y + k < NY)
        def _():
            xcol_copy(k).wait_recv()
            for j in range(1, NX):
                tile_copy(j, k).wait_recv()
            here = split(held[k])
            mirror_out[k] = multiply(here, (xrow_high[...], xrow_low[...]), TURNED)
            mirror_copy(k).start()
            total[...] += multiply(here, split(xcol[k]), PLAIN)

        return carry

    lax.fori_loop(0, NY - 1, step, 0)

    for j in range(1, NX):

        @pl.when(x - j >= 0)
        def _():
            tile_copy(j, 0).wait_recv()

    total[...] += multiply(split(held[0]), x_own, PLAIN)
    for j in range(1, NX):
        direct_copy(j).start()
    held[0, block(x)] = jnp.zeros((order, order), jnp.float32)
    out[...] = total[block(x)] + multiply(split(held[0]), (xrow_high[...], xrow_low[...]), TURNED)

    @pl.when(g < groups - 1)
    def _():
        back_copy().wait_recv()
        out[...] += multiply(split(own[slots - 1]), split(x_next[...]), PLAIN)

    @pl.when(g > 0)
    def _():
        up_copy().wait_recv()
        out[...] += up_in[...]

    def take(i, carry):
        k = step_of(i)

        @pl.when(k <= y)
        def _():
            mirror_copy(k).wait_recv()
            out[...] += mirror_in[k]

        return carry

    lax.fori_loop(0, NY - 1, take, 0)
    for j in range(1, NX):
        direct_copy(j).wait_recv()
        out[...] += direct_in[j]

    for j in range(1, NX):
        xrow_copy(j).wait_send()
        direct_copy(j).wait_send()

        @pl.when(x + j < NX)
        def _():
            tile_copy(j, 0).wait_send()

    def finish(k, carry):
        @pl.when(k <= y)
        def _():
            xcol_copy(k).wait_send()

        @pl.when(y + k < NY)
        def _():
            mirror_copy(k).wait_send()
            for j in range(1, NX):
                tile_copy(j, k).wait_send()

        return carry

    lax.fori_loop(1, NY, finish, 0)

    @pl.when(g > 0)
    def _():
        back_copy().wait_send()

    @pl.when(g < groups - 1)
    def _():
        up_copy().wait_send()


def per_device(stored_tiles, tile_flags, orbitals):
    slots, order = stored_tiles.shape[1:3]
    columns = orbitals.shape[1]
    f32, bf16 = jnp.float32, jnp.bfloat16
    dma = pltpu.SemaphoreType.DMA
    return pl.pallas_call(
        kernel,
        out_shape=jax.ShapeDtypeStruct(orbitals.shape, f32),
        in_specs=[
            pl.BlockSpec(memory_space=pl.ANY),
            pl.BlockSpec(memory_space=pltpu.SMEM),
            pl.BlockSpec(memory_space=pl.ANY),
        ],
        out_specs=pl.BlockSpec(memory_space=pltpu.VMEM),
        scratch_shapes=[
            pltpu.VMEM((slots, order, order), f32),
            pltpu.VMEM((NY, NX * order, order), f32),
            pltpu.VMEM((NX * order, columns), f32),
            pltpu.VMEM((NX * order, columns), bf16),
            pltpu.VMEM((NX * order, columns), bf16),
            pltpu.VMEM((NY, order, columns), f32),
            pltpu.VMEM((NX * order, columns), f32),
            pltpu.VMEM((NY, order, columns), f32),
            pltpu.VMEM((NY, order, columns), f32),
            pltpu.VMEM((NX, order, columns), f32),
            pltpu.VMEM((order, columns), f32),
            pltpu.VMEM((order, columns), f32),
            pltpu.VMEM((order, columns), f32),
            dma((3,)),
            dma((NX, NY)),
            dma((NX, NY)),
            dma((NX,)),
            dma((NX,)),
            dma((NY,)),
            dma((NY,)),
            dma((NY,)),
            dma((NY,)),
            dma((NX,)),
            dma((NX,)),
            dma((2,)),
            dma((2,)),
        ],
        compiler_params=pltpu.CompilerParams(
            collective_id=0, has_side_effects=True, vmem_limit_bytes=63 << 20
        ),
    )(stored_tiles[0], tile_flags, orbitals)


def solution(mesh):
    in_specs = (
        P(("grp", "dev"), None, None, None),
        P(("grp", "dev"), None),
        P(("grp", "dev"), None),
    )
    out_specs = P(("grp", "dev"), None)
    return jax.shard_map(
        per_device, mesh=mesh, in_specs=in_specs, out_specs=out_specs, check_vma=False
    )
```

```python
import jax
import jax.numpy as jnp
from jax import lax
from jax.experimental import pallas as pl
from jax.experimental.pallas import tpu as pltpu
from jax.sharding import PartitionSpec as P

MESH = pl.DeviceIdType.MESH
NX = 4
NY = 8
HALF = NY // 2
MIDDLE = HALF - 1
TILE_ORDER = (4, 5, 3, 6, 2, 1)
WINDOW = 3


TURNED_STEPS = (1, NY - 1)
TURNED_ROWS = 2


def turned(y, k):
    return (y >= 0) & (y + k < NY) & ((k == NY - 1) | ((k == 1) & (y < TURNED_ROWS)))


def straight(y, k):
    return (y >= 0) & (y + k < NY) & (k >= 1) & (turned(y, k) ^ True)


def passed(y, k):
    return straight(y, k) & (((k < HALF) & (y >= 1) & (y != HALF)) | (k > HALF + 1))


def forwards(y, k):
    return (y + k < NY) & (k <= HALF) & (y >= (2 if k == HALF else 1))


def sent_units(y):
    steps = sum(bool(straight(y, k)) for k in range(1, NY))
    given = sum(bool(turned(y, k)) for k in TURNED_STEPS)
    taken = sum(bool(turned(y - k, k)) for k in TURNED_STEPS)
    down = sum(bool(forwards(y, k)) for k in range(1, HALF + 1))
    along_row = (NX - 1) * (2 + 2 + steps)
    along_column = 2 * ((y >= 2) + (y > HALF) + down + steps + taken) + (NX + 2) * given
    return along_row, along_column


def split(v):
    high = v.astype(jnp.bfloat16)
    return high, (v - high.astype(jnp.float32)).astype(jnp.bfloat16)


def multiply(a, b, dims):
    def one(u, v):
        return lax.dot_general(u, v, (dims, ((), ())), preferred_element_type=jnp.float32)

    return one(a[0], b[0]) + (one(a[0], b[1]) + one(a[1], b[0]))


PLAIN = ((1,), (0,))
TURNED = ((0,), (0,))


def kernel(
    tiles, flags, orb, out,
    own, held, xrow, xrow_high, xrow_low, xcol, total, mirror_out, mirror_in, direct_in, x_next, up_out, up_in,
    flags_here, turned_tiles, turned_x, back_out, back_in,
    load_sem, row_send, column_send, next_send,
    tile_recv, xrow_recv, xcol_recv, mirror_recv, direct_recv, next_recv, turned_recv, token,
):
    order = tiles.shape[1]
    slots = tiles.shape[0]
    groups = lax.axis_size("grp")
    g, d = lax.axis_index("grp"), lax.axis_index("dev")
    y, x = d // NX, d % NX

    def in_row(j):
        return {"dev": y * NX + (x + j) % NX}

    def in_column(k):
        return {"dev": (y + k) * NX + x}

    def block(i):
        return pl.ds(pl.multiple_of(i * order, order), order)

    def remote(src, dst, send, recv, device):
        return pltpu.make_async_remote_copy(
            src_ref=src, dst_ref=dst, send_sem=send, recv_sem=recv, device_id=device, device_id_type=MESH
        )

    def tile_copy(j, k):
        return remote(
            own.at[(y + k) * NX + (x + j) % NX], held.at[k, block(x)],
            row_send.at[0], tile_recv.at[k - 1], in_row(j),
        )

    def done(units, send, recv):
        return remote(own.at[pl.ds(0, units)], own.at[pl.ds(0, units)], send, recv, in_row(1))

    def xrow_copy(j):
        return remote(orb, xrow.at[block(x)], row_send.at[0], xrow_recv.at[0], in_row(j))

    def at(row):
        return {"dev": row * NX + x}

    def half(ref, h):
        return ref.at[pl.ds(h * (order // 2), order // 2)]

    def xcol_send_half(src, k, h, row):
        return remote(half(src, h), half(xcol.at[k], h), column_send.at[0], xcol_recv.at[k - 1, h], at(row))

    def xcol_first(h):
        return xcol_send_half(orb, 1, h, y - 1)

    def xcol_round(h):
        first = y < NY - 1
        return xcol_send_half(orb, jnp.where(first, y, y - 1), h, jnp.where(first, 0, 1))

    def xcol_down(k, h):
        return xcol_send_half(xcol.at[k], k + 1, h, y - 1)

    def xcol_arrival(k, h):
        return xcol_send_half(orb, k, h, y)

    def forward_down(k):
        for h in range(2):

            @pl.when(forwards(y, k))
            def _():
                xcol_arrival(k, h).wait_recv()
                xcol_down(k, h).start()

    def mirror_copy(k):
        if k <= HALF:
            on, beyond = passed(y + 1, k - 1), y + 1
            place = jnp.where(on, k - 1, jnp.where((y == MIDDLE) & (k > 1), HALF + 1, 0))
        else:
            on, beyond, place = passed(y - 1, k + 1), y - 1, HALF
        row = jnp.where(on, beyond, y + k)
        return remote(mirror_out.at[k], mirror_in.at[place], column_send.at[0], mirror_recv.at[place], at(row))

    def mirror_arrival(i):
        return remote(orb, mirror_in.at[i], column_send.at[0], mirror_recv.at[i], at(y))

    def direct_copy(j):
        return remote(
            total.at[block((x + j) % NX)], direct_in.at[j], row_send.at[0], direct_recv.at[0], in_row(j)
        )

    def back_copy():
        return remote(orb, x_next, next_send.at[0], next_recv.at[0], {"grp": g - 1})

    def up_copy():
        return remote(up_out, up_in, next_send.at[1], next_recv.at[1], {"grp": g + 1})

    def turned_tile_copy(e, k):
        return remote(
            own.at[pl.ds((y + k) * NX, NX)], turned_tiles.at[e], column_send.at[0], turned_recv.at[0], in_column(k)
        )

    def turned_x_copy(e, k):
        return remote(orb, turned_x.at[e], column_send.at[0], turned_recv.at[0], in_column(k))

    def turned_back_copy(e, k):
        return remote(back_out.at[e], back_in.at[e], column_send.at[0], turned_recv.at[1 + e], in_column(-k))

    load_tiles = pltpu.make_async_copy(tiles, own, load_sem.at[0])
    load_row = pltpu.make_async_copy(orb, xrow.at[block(x)], load_sem.at[1])
    load_col = pltpu.make_async_copy(orb, xcol.at[0], load_sem.at[2])
    load_flags = pltpu.make_async_copy(flags, flags_here, load_sem.at[3])
    load_flags.start()
    load_tiles.start()
    load_row.start()
    load_col.start()

    def greet(condition, semaphore, row):
        @pl.when(condition)
        def _():
            pl.semaphore_signal(semaphore, inc=1, device_id=at(row), device_id_type=MESH)

    barrier = pltpu.get_barrier_semaphore()
    for j in range(1, NX):
        pl.semaphore_signal(barrier, inc=1, device_id=in_row(j), device_id_type=MESH)
    greet(y > 0, barrier, y - 1)
    greet(y < NY - 1, barrier, y + 1)
    greet(y > HALF, barrier, MIDDLE)
    for row in range(HALF + 1, NY):
        greet(y == MIDDLE, barrier, row)

    @pl.when(g > 0)
    def _():
        pl.semaphore_signal(barrier, inc=1, device_id={"grp": g - 1}, device_id_type=MESH)

    @pl.when(g < groups - 1)
    def _():
        pl.semaphore_signal(barrier, inc=1, device_id={"grp": g + 1}, device_id_type=MESH)

    load_flags.wait()
    load_tiles.wait()

    def mask(s, carry):
        own[s] = own[s] * flags_here[0, s].astype(jnp.float32)
        return carry

    lax.fori_loop(y * NX, slots, mask, 0)

    peers = NX - 1
    for condition in (g > 0, g < groups - 1, y > 0, y < NY - 1, y > HALF):
        peers = peers + condition.astype(jnp.int32)
    peers = peers + jnp.where(y == MIDDLE, NY - 1 - HALF, 0)
    pl.semaphore_wait(barrier, peers)

    @pl.when(y >= 2)
    def _():
        xcol_first(0).start()
        xcol_first(1).start()

    for j in (2, 1, 3):
        xrow_copy(j).start()

    @pl.when(turned(y, 1))
    def _():
        turned_tile_copy(0, 1).start()
        turned_x_copy(0, 1).start()

    @pl.when(g > 0)
    def _():
        back_copy().start()

    def send_tiles(k):
        @pl.when(straight(y, k))
        def _():
            for j in (2, 1, 3):
                tile_copy(j, k).start()

    for k in TILE_ORDER[:WINDOW]:
        send_tiles(k)

    greet(y == 0, token.at[0], 1)
    greet(y == MIDDLE, token.at[1], MIDDLE - 1)

    @pl.when((y > 0) & (y <= MIDDLE))
    def _():
        pl.semaphore_wait(token.at[0], 1)

    greet((y > 0) & (y < MIDDLE), token.at[0], y + 1)
    for row in range(HALF + 1, NY):
        greet(y == MIDDLE, token.at[0], row)

    load_row.wait()
    load_col.wait()
    x_own = split(xcol[0])

    @pl.when(g < groups - 1)
    def _():
        up_out[...] = multiply(split(own[slots - 1]), x_own, TURNED)
        up_copy().start()

    def place(k, carry):
        held[k, block(x)] = own[(y + k) * NX + x]
        return carry

    lax.fori_loop(1, NY - y, place, 0)
    beside = jnp.concatenate([own[y * NX + b] for b in range(NX)], axis=1)
    column = lax.broadcasted_iota(jnp.int32, beside.shape, 1)
    total[...] = multiply(
        split(jnp.where(column // order == x, 0.0, beside)), x_own, TURNED
    )
    forward_down(1)

    @pl.when(y < MIDDLE)
    def _():
        pl.semaphore_wait(token.at[1], 1)

    greet((y > 0) & (y < MIDDLE), token.at[1], y - 1)

    @pl.when(turned(y, NY - 1))
    def _():
        turned_tile_copy(1, NY - 1).start()
        turned_x_copy(1, NY - 1).start()

    forward_down(2)

    @pl.when(y > HALF)
    def _():
        pl.semaphore_wait(token.at[0], 1)
        xcol_round(0).start()
        xcol_round(1).start()

    forward_down(3)
    done(2 * (NX - 1), row_send.at[0], xrow_recv.at[0]).wait_recv()
    xrow_high[...], xrow_low[...] = split(xrow[...])
    out[...] = multiply(split(beside), (xrow_high[...], xrow_low[...]), PLAIN)

    def await_tiles(k):
        @pl.when(straight(y, k))
        def _():
            done(NX - 1, row_send.at[0], tile_recv.at[k - 1]).wait_recv()

        later = TILE_ORDER.index(k) + WINDOW
        if later < len(TILE_ORDER):
            send_tiles(TILE_ORDER[later])

    def mirror_step(k):
        @pl.when(straight(y, k))
        def _():
            mirror_out[k] = multiply(split(held[k]), (xrow_high[...], xrow_low[...]), TURNED)

    def pass_step(k):
        @pl.when(passed(y, k))
        def _():
            mirror_arrival(min(k, HALF)).wait_recv()
            mirror_out[k] += mirror_in[min(k, HALF)]

        @pl.when(straight(y, k))
        def _():
            mirror_copy(k).start()

    def direct_step(k):
        @pl.when(straight(y, k) & (forwards(y, k) ^ True))
        def _():
            xcol_arrival(k, 0).wait_recv()
            xcol_arrival(k, 1).wait_recv()

        @pl.when(straight(y, k))
        def _():
            total[...] += multiply(split(held[k]), split(xcol[k]), PLAIN)

    def send_direct():
        for j in (2, 1, 3):
            direct_copy(j).start()

    for k in (4, 5):
        await_tiles(k)
        mirror_step(k)
        pass_step(k)
        if k == HALF:
            forward_down(4)
    for e, k in enumerate(TURNED_STEPS):

        @pl.when(turned(y - k, k))
        def _():
            done(NX + 2, column_send.at[0], turned_recv.at[0]).wait_recv()
            wide = split(jnp.concatenate([turned_tiles[e, b] for b in range(NX)], axis=1))
            back_out[e] = multiply(wide, (xrow_high[...], xrow_low[...]), PLAIN)
            turned_back_copy(e, k).start()
            total[...] += multiply(wide, split(turned_x[e]), TURNED)

    @pl.when(g < groups - 1)
    def _():
        back_copy().wait_recv()
        out[...] += multiply(split(own[slots - 1]), split(x_next[...]), PLAIN)

    @pl.when(g > 0)
    def _():
        up_copy().wait_recv()
        out[...] += up_in[...]

    await_tiles(3)
    mirror_step(3)
    pass_step(3)
    direct_step(4)
    await_tiles(6)
    mirror_step(6)
    direct_step(5)
    direct_step(3)
    direct_step(6)
    await_tiles(2)
    mirror_step(2)
    pass_step(2)
    direct_step(2)

    @pl.when(y < TURNED_ROWS)
    def _():
        send_direct()

    pass_step(6)
    await_tiles(1)
    direct_step(1)

    @pl.when(y >= TURNED_ROWS)
    def _():
        send_direct()

    mirror_step(1)
    pass_step(1)
    out[...] += total[block(x)]

    for e, k in enumerate(TURNED_STEPS):

        @pl.when(turned(y, k))
        def _():
            turned_back_copy(e, k).wait_recv()
            out[...] += back_in[e]

    @pl.when(y > HALF)
    def _():
        mirror_arrival(HALF).wait_recv()
        mirror_arrival(HALF + 1).wait_recv()
        out[...] += mirror_in[HALF] + mirror_in[HALF + 1]

    @pl.when(y >= 2)
    def _():
        mirror_arrival(0).wait_recv()
        out[...] += mirror_in[0]

    done(2 * (NX - 1), row_send.at[0], direct_recv.at[0]).wait_recv()
    out[...] += direct_in[1] + direct_in[2] + direct_in[3]

    for row in range(NY):

        @pl.when(y == row)
        def _():
            along_row, along_column = sent_units(row)
            done(along_row, row_send.at[0], xrow_recv.at[0]).wait_send()
            done(along_column, column_send.at[0], xrow_recv.at[0]).wait_send()

    @pl.when(g > 0)
    def _():
        back_copy().wait_send()

    @pl.when(g < groups - 1)
    def _():
        up_copy().wait_send()


def per_device(stored_tiles, tile_flags, orbitals):
    slots, order = stored_tiles.shape[1:3]
    columns = orbitals.shape[1]
    f32, bf16 = jnp.float32, jnp.bfloat16
    dma = pltpu.SemaphoreType.DMA
    return pl.pallas_call(
        kernel,
        out_shape=jax.ShapeDtypeStruct(orbitals.shape, f32),
        in_specs=[pl.BlockSpec(memory_space=pl.ANY)] * 3,
        out_specs=pl.BlockSpec(memory_space=pltpu.VMEM),
        scratch_shapes=[
            pltpu.VMEM((slots, order, order), f32),
            pltpu.VMEM((NY, NX * order, order), f32),
            pltpu.VMEM((NX * order, columns), f32),
            pltpu.VMEM((NX * order, columns), bf16),
            pltpu.VMEM((NX * order, columns), bf16),
            pltpu.VMEM((NY, order, columns), f32),
            pltpu.VMEM((NX * order, columns), f32),
            pltpu.VMEM((NY, order, columns), f32),
            pltpu.VMEM((HALF + 2, order, columns), f32),
            pltpu.VMEM((NX, order, columns), f32),
            pltpu.VMEM((order, columns), f32),
            pltpu.VMEM((order, columns), f32),
            pltpu.VMEM((order, columns), f32),
            pltpu.SMEM(tile_flags.shape, jnp.int32),
            pltpu.VMEM((2, NX, order, order), f32),
            pltpu.VMEM((2, order, columns), f32),
            pltpu.VMEM((2, order, columns), f32),
            pltpu.VMEM((2, order, columns), f32),
            dma((4,)),
            dma((1,)),
            dma((1,)),
            dma((2,)),
            dma((NY - 2,)),
            dma((1,)),
            dma((NY - 2, 2)),
            dma((HALF + 2,)),
            dma((1,)),
            dma((2,)),
            dma((3,)),
            pltpu.SemaphoreType.REGULAR((2,)),
        ],
        compiler_params=pltpu.CompilerParams(
            collective_id=0, has_side_effects=True, vmem_limit_bytes=48 << 20
        ),
    )(*(pltpu.with_memory_space_constraint(v, pltpu.HBM) for v in (stored_tiles[0], tile_flags, orbitals)))


def solution(mesh):
    in_specs = (
        P(("grp", "dev"), None, None, None),
        P(("grp", "dev"), None),
        P(("grp", "dev"), None),
    )
    out_specs = P(("grp", "dev"), None)
    return jax.shard_map(
        per_device, mesh=mesh, in_specs=in_specs, out_specs=out_specs, check_vma=False
    )
```

```python
import jax
import jax.numpy as jnp
from jax import lax
from jax.experimental import pallas as pl
from jax.experimental.pallas import tpu as pltpu
from jax.sharding import PartitionSpec as P

MESH = pl.DeviceIdType.MESH
NX = 4
NY = 8
HALF = NY // 2
MIDDLE = HALF - 1
TILE_ORDER = (4, 5, 3, 6, 2, 1)
WINDOW = 4


TURNED_STEPS = (1, NY - 1)
TURNED_ROWS = 2


def turned(y, k):
    return (y >= 0) & (y + k < NY) & ((k == NY - 1) | ((k == 1) & (y < TURNED_ROWS)))


def straight(y, k):
    return (y >= 0) & (y + k < NY) & (k >= 1) & (turned(y, k) ^ True)


def passed(y, k):
    return straight(y, k) & (((k < HALF) & (y >= 1) & (y != HALF)) | (k > HALF + 1))


def forwards(y, k):
    return (y + k < NY) & (k <= HALF) & (y >= (2 if k == HALF else 1))


def sent_units(y):
    steps = sum(bool(straight(y, k)) for k in range(1, NY))
    given = sum(bool(turned(y, k)) for k in TURNED_STEPS)
    taken = sum(bool(turned(y - k, k)) for k in TURNED_STEPS)
    down = sum(bool(forwards(y, k)) for k in range(1, HALF + 1))
    along_row = (NX - 1) * (2 + 2 + steps)
    along_column = 2 * ((y >= 2) + (y > HALF) + down + steps + taken) + (NX + 2) * given
    return along_row, along_column


def split(v):
    high = v.astype(jnp.bfloat16)
    return high, (v - high.astype(jnp.float32)).astype(jnp.bfloat16)


def multiply(a, b, dims):
    def one(u, v):
        return lax.dot_general(u, v, (dims, ((), ())), preferred_element_type=jnp.float32)

    return one(a[0], b[0]) + (one(a[0], b[1]) + one(a[1], b[0]))


PLAIN = ((1,), (0,))
TURNED = ((0,), (0,))


def kernel(
    tiles, flags, orb, out,
    own, held, xrow, xrow_high, xrow_low, xcol, total, mirror_out, mirror_in, direct_in, x_next, up_out, up_in,
    flags_here, turned_tiles, turned_x, back_out, back_in,
    load_sem, row_send, column_send, next_send,
    tile_recv, xrow_recv, xcol_recv, mirror_recv, direct_recv, next_recv, turned_recv, token,
):
    order = tiles.shape[1]
    slots = tiles.shape[0]
    groups = lax.axis_size("grp")
    g, d = lax.axis_index("grp"), lax.axis_index("dev")
    y, x = d // NX, d % NX

    def in_row(j):
        return {"dev": y * NX + (x + j) % NX}

    def in_column(k):
        return {"dev": (y + k) * NX + x}

    def block(i):
        return pl.ds(pl.multiple_of(i * order, order), order)

    def remote(src, dst, send, recv, device):
        return pltpu.make_async_remote_copy(
            src_ref=src, dst_ref=dst, send_sem=send, recv_sem=recv, device_id=device, device_id_type=MESH
        )

    def tile_copy(j, k):
        return remote(
            own.at[(y + k) * NX + (x + j) % NX], held.at[k, block(x)],
            row_send.at[0], tile_recv.at[k - 1], in_row(j),
        )

    def done(units, send, recv):
        return remote(own.at[pl.ds(0, units)], own.at[pl.ds(0, units)], send, recv, in_row(1))

    def xrow_copy(j):
        return remote(orb, xrow.at[block(x)], row_send.at[0], xrow_recv.at[0], in_row(j))

    def at(row):
        return {"dev": row * NX + x}

    def half(ref, h):
        return ref.at[pl.ds(h * (order // 2), order // 2)]

    def xcol_send_half(src, k, h, row):
        return remote(half(src, h), half(xcol.at[k], h), column_send.at[0], xcol_recv.at[k - 1, h], at(row))

    def xcol_first(h):
        return xcol_send_half(orb, 1, h, y - 1)

    def xcol_round(h):
        first = y < NY - 1
        return xcol_send_half(orb, jnp.where(first, y, y - 1), h, jnp.where(first, 0, 1))

    def xcol_down(k, h):
        return xcol_send_half(xcol.at[k], k + 1, h, y - 1)

    def xcol_arrival(k, h):
        return xcol_send_half(orb, k, h, y)

    def forward_down(k):
        for h in range(2):

            @pl.when(forwards(y, k))
            def _():
                xcol_arrival(k, h).wait_recv()
                xcol_down(k, h).start()

    def mirror_copy(k):
        if k <= HALF:
            on, beyond = passed(y + 1, k - 1), y + 1
            place = jnp.where(on, k - 1, jnp.where((y == MIDDLE) & (k > 1), HALF + 1, 0))
        else:
            on, beyond, place = passed(y - 1, k + 1), y - 1, HALF
        row = jnp.where(on, beyond, y + k)
        return remote(mirror_out.at[k], mirror_in.at[place], column_send.at[0], mirror_recv.at[place], at(row))

    def mirror_arrival(i):
        return remote(orb, mirror_in.at[i], column_send.at[0], mirror_recv.at[i], at(y))

    def direct_copy(j):
        return remote(
            total.at[block((x + j) % NX)], direct_in.at[j], row_send.at[0], direct_recv.at[0], in_row(j)
        )

    def back_copy():
        return remote(orb, x_next, next_send.at[0], next_recv.at[0], {"grp": g - 1})

    def up_copy():
        return remote(up_out, up_in, next_send.at[1], next_recv.at[1], {"grp": g + 1})

    def turned_tile_copy(e, k):
        return remote(
            own.at[pl.ds((y + k) * NX, NX)], turned_tiles.at[e], column_send.at[0], turned_recv.at[0], in_column(k)
        )

    def turned_x_copy(e, k):
        return remote(orb, turned_x.at[e], column_send.at[0], turned_recv.at[0], in_column(k))

    def turned_back_copy(e, k):
        return remote(back_out.at[e], back_in.at[e], column_send.at[0], turned_recv.at[1 + e], in_column(-k))

    load_tiles = pltpu.make_async_copy(tiles, own, load_sem.at[0])
    load_row = pltpu.make_async_copy(orb, xrow.at[block(x)], load_sem.at[1])
    load_col = pltpu.make_async_copy(orb, xcol.at[0], load_sem.at[2])
    load_flags = pltpu.make_async_copy(flags, flags_here, load_sem.at[3])
    load_flags.start()
    load_tiles.start()
    load_row.start()
    load_col.start()

    def greet(condition, semaphore, row):
        @pl.when(condition)
        def _():
            pl.semaphore_signal(semaphore, inc=1, device_id=at(row), device_id_type=MESH)

    barrier = pltpu.get_barrier_semaphore()
    for j in range(1, NX):
        pl.semaphore_signal(barrier, inc=1, device_id=in_row(j), device_id_type=MESH)
    greet(y > 0, barrier, y - 1)
    greet(y < NY - 1, barrier, y + 1)
    greet(y > HALF, barrier, MIDDLE)
    for row in range(HALF + 1, NY):
        greet(y == MIDDLE, barrier, row)

    @pl.when(g > 0)
    def _():
        pl.semaphore_signal(barrier, inc=1, device_id={"grp": g - 1}, device_id_type=MESH)

    @pl.when(g < groups - 1)
    def _():
        pl.semaphore_signal(barrier, inc=1, device_id={"grp": g + 1}, device_id_type=MESH)

    load_flags.wait()
    load_tiles.wait()

    def mask(s, carry):
        own[s] = own[s] * flags_here[0, s].astype(jnp.float32)
        return carry

    lax.fori_loop(y * NX, slots, mask, 0)

    peers = NX - 1
    for condition in (g > 0, g < groups - 1, y > 0, y < NY - 1, y > HALF):
        peers = peers + condition.astype(jnp.int32)
    peers = peers + jnp.where(y == MIDDLE, NY - 1 - HALF, 0)
    pl.semaphore_wait(barrier, peers)

    @pl.when(y >= 2)
    def _():
        xcol_first(0).start()
        xcol_first(1).start()

    for j in (2, 1, 3):
        xrow_copy(j).start()

    @pl.when(turned(y, 1))
    def _():
        turned_tile_copy(0, 1).start()
        turned_x_copy(0, 1).start()

    @pl.when(g > 0)
    def _():
        back_copy().start()

    def send_tiles(k):
        @pl.when(straight(y, k))
        def _():
            for j in (2, 1, 3):
                tile_copy(j, k).start()

    for k in TILE_ORDER[:WINDOW]:
        send_tiles(k)

    greet(y == 0, token.at[0], 1)
    greet(y == MIDDLE, token.at[1], MIDDLE - 1)

    @pl.when((y > 0) & (y <= MIDDLE))
    def _():
        pl.semaphore_wait(token.at[0], 1)

    greet((y > 0) & (y < MIDDLE), token.at[0], y + 1)
    for row in range(HALF + 1, NY):
        greet(y == MIDDLE, token.at[0], row)

    load_row.wait()
    load_col.wait()
    x_own = split(xcol[0])

    @pl.when(g < groups - 1)
    def _():
        up_out[...] = multiply(split(own[slots - 1]), x_own, TURNED)
        up_copy().start()

    def place(k, carry):
        held[k, block(x)] = own[(y + k) * NX + x]
        return carry

    lax.fori_loop(1, NY - y, place, 0)
    beside = jnp.concatenate([own[y * NX + b] for b in range(NX)], axis=1)
    column = lax.broadcasted_iota(jnp.int32, beside.shape, 1)
    total[...] = multiply(
        split(jnp.where(column // order == x, 0.0, beside)), x_own, TURNED
    )
    forward_down(1)

    @pl.when(y < MIDDLE)
    def _():
        pl.semaphore_wait(token.at[1], 1)

    greet((y > 0) & (y < MIDDLE), token.at[1], y - 1)

    @pl.when(turned(y, NY - 1))
    def _():
        turned_tile_copy(1, NY - 1).start()
        turned_x_copy(1, NY - 1).start()

    forward_down(2)

    @pl.when(y > HALF)
    def _():
        pl.semaphore_wait(token.at[0], 1)
        xcol_round(0).start()
        xcol_round(1).start()

    forward_down(3)
    done(2 * (NX - 1), row_send.at[0], xrow_recv.at[0]).wait_recv()
    xrow_high[...], xrow_low[...] = split(xrow[...])
    out[...] = multiply(split(beside), (xrow_high[...], xrow_low[...]), PLAIN)

    def await_tiles(k):
        @pl.when(straight(y, k))
        def _():
            done(NX - 1, row_send.at[0], tile_recv.at[k - 1]).wait_recv()

        later = TILE_ORDER.index(k) + WINDOW
        if later < len(TILE_ORDER):
            send_tiles(TILE_ORDER[later])

    def mirror_step(k):
        @pl.when(straight(y, k))
        def _():
            mirror_out[k] = multiply(split(held[k]), (xrow_high[...], xrow_low[...]), TURNED)

    def pass_step(k):
        @pl.when(passed(y, k))
        def _():
            mirror_arrival(min(k, HALF)).wait_recv()
            mirror_out[k] += mirror_in[min(k, HALF)]

        @pl.when(straight(y, k))
        def _():
            mirror_copy(k).start()

    def direct_step(k):
        @pl.when(straight(y, k) & (forwards(y, k) ^ True))
        def _():
            xcol_arrival(k, 0).wait_recv()
            xcol_arrival(k, 1).wait_recv()

        @pl.when(straight(y, k))
        def _():
            total[...] += multiply(split(held[k]), split(xcol[k]), PLAIN)

    def send_direct():
        for j in (2, 1, 3):
            direct_copy(j).start()

    for k in (4, 5):
        await_tiles(k)
        mirror_step(k)
        pass_step(k)
        if k == HALF:
            forward_down(4)
    for e, k in enumerate(TURNED_STEPS):

        @pl.when(turned(y - k, k))
        def _():
            done(NX + 2, column_send.at[0], turned_recv.at[0]).wait_recv()
            wide = split(jnp.concatenate([turned_tiles[e, b] for b in range(NX)], axis=1))
            back_out[e] = multiply(wide, (xrow_high[...], xrow_low[...]), PLAIN)
            turned_back_copy(e, k).start()
            total[...] += multiply(wide, split(turned_x[e]), TURNED)

    @pl.when(g < groups - 1)
    def _():
        back_copy().wait_recv()
        out[...] += multiply(split(own[slots - 1]), split(x_next[...]), PLAIN)

    @pl.when(g > 0)
    def _():
        up_copy().wait_recv()
        out[...] += up_in[...]

    await_tiles(3)
    mirror_step(3)
    pass_step(3)
    direct_step(4)
    await_tiles(6)
    mirror_step(6)
    direct_step(5)
    direct_step(3)
    direct_step(6)
    await_tiles(2)
    mirror_step(2)
    pass_step(2)
    direct_step(2)

    @pl.when(y < TURNED_ROWS)
    def _():
        send_direct()

    pass_step(6)
    await_tiles(1)
    direct_step(1)

    @pl.when(y >= TURNED_ROWS)
    def _():
        send_direct()

    mirror_step(1)
    pass_step(1)
    out[...] += total[block(x)]

    for e, k in enumerate(TURNED_STEPS):

        @pl.when(turned(y, k))
        def _():
            turned_back_copy(e, k).wait_recv()
            out[...] += back_in[e]

    @pl.when(y > HALF)
    def _():
        mirror_arrival(HALF).wait_recv()
        mirror_arrival(HALF + 1).wait_recv()
        out[...] += mirror_in[HALF] + mirror_in[HALF + 1]

    @pl.when(y >= 2)
    def _():
        mirror_arrival(0).wait_recv()
        out[...] += mirror_in[0]

    done(2 * (NX - 1), row_send.at[0], direct_recv.at[0]).wait_recv()
    out[...] += direct_in[1] + direct_in[2] + direct_in[3]

    for row in range(NY):

        @pl.when(y == row)
        def _():
            along_row, along_column = sent_units(row)
            done(along_row, row_send.at[0], xrow_recv.at[0]).wait_send()
            done(along_column, column_send.at[0], xrow_recv.at[0]).wait_send()

    @pl.when(g > 0)
    def _():
        back_copy().wait_send()

    @pl.when(g < groups - 1)
    def _():
        up_copy().wait_send()


def per_device(stored_tiles, tile_flags, orbitals):
    slots, order = stored_tiles.shape[1:3]
    columns = orbitals.shape[1]
    f32, bf16 = jnp.float32, jnp.bfloat16
    dma = pltpu.SemaphoreType.DMA
    return pl.pallas_call(
        kernel,
        out_shape=jax.ShapeDtypeStruct(orbitals.shape, f32),
        in_specs=[pl.BlockSpec(memory_space=pl.ANY)] * 3,
        out_specs=pl.BlockSpec(memory_space=pltpu.VMEM),
        scratch_shapes=[
            pltpu.VMEM((slots, order, order), f32),
            pltpu.VMEM((NY, NX * order, order), f32),
            pltpu.VMEM((NX * order, columns), f32),
            pltpu.VMEM((NX * order, columns), bf16),
            pltpu.VMEM((NX * order, columns), bf16),
            pltpu.VMEM((NY, order, columns), f32),
            pltpu.VMEM((NX * order, columns), f32),
            pltpu.VMEM((NY, order, columns), f32),
            pltpu.VMEM((HALF + 2, order, columns), f32),
            pltpu.VMEM((NX, order, columns), f32),
            pltpu.VMEM((order, columns), f32),
            pltpu.VMEM((order, columns), f32),
            pltpu.VMEM((order, columns), f32),
            pltpu.SMEM(tile_flags.shape, jnp.int32),
            pltpu.VMEM((2, NX, order, order), f32),
            pltpu.VMEM((2, order, columns), f32),
            pltpu.VMEM((2, order, columns), f32),
            pltpu.VMEM((2, order, columns), f32),
            dma((4,)),
            dma((1,)),
            dma((1,)),
            dma((2,)),
            dma((NY - 2,)),
            dma((1,)),
            dma((NY - 2, 2)),
            dma((HALF + 2,)),
            dma((1,)),
            dma((2,)),
            dma((3,)),
            pltpu.SemaphoreType.REGULAR((2,)),
        ],
        compiler_params=pltpu.CompilerParams(
            collective_id=0, has_side_effects=True, vmem_limit_bytes=48 << 20
        ),
    )(*(pltpu.with_memory_space_constraint(v, pltpu.HBM) for v in (stored_tiles[0], tile_flags, orbitals)))


def solution(mesh):
    in_specs = (
        P(("grp", "dev"), None, None, None),
        P(("grp", "dev"), None),
        P(("grp", "dev"), None),
    )
    out_specs = P(("grp", "dev"), None)
    return jax.shard_map(
        per_device, mesh=mesh, in_specs=in_specs, out_specs=out_specs, check_vma=False
    )
```
